256 devices in a mesh: fsdp: 32 (over x, z_lo, core), dp: 8 (over y, z_hi).
Axes of the slice: x: 4, y: 4, z: 8 (z_hi: 2, z_lo: 4; z = z_hi * 4 + z_lo), core: 2. Of those that a mesh axis runs over, the one named last changes fastest.
Arguments:
- tokens: bfloat16 [32768, 4096], P(('fsdp', 'dp')), may hold values from -6 to 6
- owner: int32 [32768, 4], P(('fsdp', 'dp')), may hold values from 0 to 31, all different within a row; in each aligned block of 128 rows (0 to 127, 128 to 255, ...) at most 24 rows name the same one
- row_pick: int32 [32768, 4, 32], P(('fsdp', 'dp')), may hold values from 0 to 255, as said below
- query_weight: bfloat16 [4096, 512], P('fsdp'), may hold values from -0.09375 to 0.09375
- sub_keys: bfloat16 [4, 256, 128], replicated, may hold values from -2000 to 2000
- values: bfloat16 [8192, 4096], P('fsdp'), may hold values from -6 to 6
- cotangent: bfloat16 [32768, 4096], P(('fsdp', 'dp')), may hold values from -6 to 6
Outputs:
- memory_out: bfloat16 [32768, 4096], P(('fsdp', 'dp'))
- grad_values: bfloat16 [8192, 4096], P(('fsdp', 'dp'))
The draws below stay inside these ranges and needn't reach their ends.
Inputs may be any that keep to these rules, and one draw needn't show every extreme that they name: `owner`: each token's 4 heads name different blocks; the 128 tokens of one device name no block more than 24 times, and some block exactly 24 times. `row_pick`: the 32 rows that one head of one token reads are distinct.
All inputs are finite; a program needn't handle non-finite values.
Results may differ from the reference program's by a relative error of at most 0.012.
The reference program's roundings to bfloat16 on the way (of `query`, `weight` and `read`) count: a program that leaves them out, or rounds other values in their place, can miss the bound.
Values may be sent and summed in bfloat16 or wider, within the bound.
No kernel may reach another device: no remote copies, remote signals or barrier semaphores. Data moves between devices by JAX's collectives and lax.ppermute only.
A program may use at most 64 MiB of HBM per device.

```python
import math
import jax
import jax.numpy as jnp
import numpy as np
from jax import lax

D = 4096
HEADS = 4
TOPK = 32
KH = 128
VROWS_DEV = 256
TOK_DEV = 128
CAP = 24
TOKENS = 32768
SLAB_ROWS = 8192
N_FSDP = 32


def draw_row_pick(key, part):
    scores = jax.random.randint(key, (TOKENS, HEADS, VROWS_DEV), 0, 2 ** 30)
    order = jnp.argsort(scores, axis=-1, stable=True)
    return order[..., :TOPK].astype(jnp.int32)


def draw_sub_keys(key, part):
    first = jax.random.fold_in(jax.random.fold_in(key, 17), 0)
    base = jax.random.normal(first, (HEADS, VROWS_DEV, KH), jnp.float32)
    base = jnp.clip(base, -6.0, 6.0)
    return base.astype(jnp.bfloat16)


def shard_levels(stream_key, extent, cuts, low, largest):
    def one(position, parts):
        steps = jax.random.uniform(jax.random.fold_in(jax.random.fold_in(stream_key, 6), position), (parts,), jnp.float32, low / len(cuts), largest / len(cuts))
        return jnp.repeat(jnp.exp(steps), extent[position] // parts).reshape((-1,) + (1,) * (len(extent) - position - 1))

    loudness = one(*cuts[0])
    for cut in cuts[1:]:
        loudness = loudness * one(*cut)
    return loudness


def routed_block(own_key, own, number, rows, number_of, top, reach, slope):
    order = jax.random.permutation(own_key, number_of)
    heavy_load, ordinary = load_shares(number_of, rows * top, reach, slope, True), load_shares(number_of, rows * top, reach, slope, False)
    places = jnp.arange(number_of)

    def named(tallies, turn):
        used = int((tallies > 0).sum())
        fixed = max(1, used // 4)
        shifted = fixed + (places - fixed + turn * (used - fixed)) % max(1, number_of - fixed)
        return jnp.zeros((number_of,), jnp.int32).at[order[jnp.where(places < fixed, places, shifted)]].set(jnp.asarray(tallies, jnp.int32))

    tallies = jnp.where(number % 4 == 0, named(heavy_load, number // 4), named(ordinary, number - number // 4 - 1))
    mixed = jax.random.permutation(jax.random.fold_in(own, 3), number_of)
    donor, sink = mixed[0:number_of // 2 * 2:2], mixed[1:number_of // 2 * 2:2]
    slack = jnp.minimum(tallies[donor] - 1, reach - tallies[sink]) // 2
    slack = jnp.where((donor == order[0]) | (sink == order[0]) | (tallies[sink] == 0), 0, jnp.maximum(slack, 0))
    shifted = jax.random.randint(jax.random.fold_in(own, 4), (number_of // 2,), 0, 1 << 20) % (slack + 1)
    tallies = tallies.at[donor].add(-shifted).at[sink].add(shifted)
    labels = jnp.searchsorted(jnp.cumsum(tallies), jnp.arange(rows * top), side="right").astype(jnp.int32)
    listing = labels.reshape(top, rows).T
    listing = listing[jax.random.permutation(jax.random.fold_in(own, 1), rows)]
    turn = jax.random.randint(jax.random.fold_in(own, 2), (rows, 1), 0, top)
    return jnp.take_along_axis(listing, (jnp.arange(top)[None, :] + turn) % top, axis=1)


def load_shares(amount, total, limit, lean, full):
    portions = [(1 << 20) // math.isqrt(grade ** lean) + 1 for grade in range(1, amount + 1)]
    largest = limit if full else min(limit, max(-(-total // amount), total * portions[0] // sum(portions)))
    least = 1 if total - largest >= amount - 1 else 0
    holding, spare = [largest] + [least] * (amount - 1), total - largest - least * (amount - 1)
    while spare > 0:
        free = [i for i in range(1, amount) if holding[i] < largest] or [i for i in range(1, amount) if holding[i] < limit]
        whole, budget = sum([portions[i] for i in free]), spare
        for i in free:
            addition = min(limit - holding[i], max(1, budget * portions[i] // whole), spare)
            holding[i] = holding[i] + addition
            spare = spare - addition
    return np.array(holding)


def scatter_about(rng, shape, spread, bound, cuts=(), held_as=jnp.bfloat16):
    level = shard_levels(rng, shape, cuts, -0.22, 0.18) if cuts else 1.0
    array = jax.random.normal(rng, shape, jnp.float32) * spread * level
    return jnp.minimum(jnp.maximum(array, -bound), bound).astype(held_as)


def setup_inputs(seed: int = 0) -> dict:
    arg_keys = jax.random.split(jax.random.key(seed), 8)
    tokens = scatter_about(arg_keys[0], (TOKENS, D), 1.0, 6.0, ((0, 256),))
    owner_keys = jax.random.split(jax.random.fold_in(arg_keys[1], 1), TOKENS // TOK_DEV)
    owner_turns = jax.random.permutation(jax.random.fold_in(arg_keys[1], 3), TOKENS // TOK_DEV)
    owner = jax.vmap(lambda own, number: routed_block(jax.random.fold_in(arg_keys[1], 2), own, number, TOK_DEV, N_FSDP, HEADS, CAP, 2))(owner_keys, owner_turns).reshape((TOKENS, HEADS))
    row_pick = draw_row_pick(jax.random.fold_in(arg_keys[7], 71), 0)
    query_weight = scatter_about(arg_keys[3], (D, HEADS * KH), D ** -0.5, 0.09375, ((0, 32),))
    sub_keys = draw_sub_keys(jax.random.fold_in(arg_keys[7], 71), 0)
    values = scatter_about(arg_keys[5], (SLAB_ROWS, D), 1.0, 6.0, ((0, 32),))
    cotangent = scatter_about(arg_keys[6], (TOKENS, D), 1.0, 6.0, ((0, 256),))
    return {"tokens": tokens, "owner": owner, "row_pick": row_pick, "query_weight": query_weight, "sub_keys": sub_keys, "values": values, "cotangent": cotangent}


def reference(tokens, owner, row_pick, query_weight, sub_keys, values, cotangent):
    query = jnp.dot(tokens, query_weight, preferred_element_type=jnp.float32).astype(jnp.bfloat16)
    query = query.reshape(TOKENS, HEADS, KH)
    full = jnp.einsum("thk,hrk->thr", query.astype(jnp.float32), sub_keys.astype(jnp.float32))
    score = jnp.take_along_axis(full, row_pick, axis=2) * (1.0 / (KH ** 0.5))
    top = jnp.max(score, axis=2, keepdims=True)
    expo = jnp.exp(score - top)
    weight = (expo / jnp.sum(expo, axis=2, keepdims=True)).astype(jnp.bfloat16)
    index = (owner[:, :, None] * VROWS_DEV + row_pick).astype(jnp.int32)
    blocks = TOKENS // TOK_DEV
    index_blocks = index.reshape(blocks, TOK_DEV, HEADS, TOPK)
    weight_blocks = weight.reshape(blocks, TOK_DEV, HEADS, TOPK)
    grad_blocks = cotangent.reshape(blocks, TOK_DEV, D)

    def read_block(pair):
        idx, wts = pair
        rows = values[idx].astype(jnp.float32)
        read = jnp.einsum("bhk,bhkd->bhd", wts.astype(jnp.float32), rows).astype(jnp.bfloat16)
        read = lax.optimization_barrier(read)
        return jnp.sum(read.astype(jnp.float32), axis=1).astype(jnp.bfloat16)

    memory_out = lax.map(read_block, (index_blocks, weight_blocks)).reshape(TOKENS, D)

    def add_block(total, trio):
        idx, wts, grd = trio
        terms = wts.astype(jnp.float32)[:, :, :, None] * grd.astype(jnp.float32)[:, None, None, :]
        return total.at[idx.reshape(-1)].add(terms.reshape(-1, D)), None

    start = jnp.zeros((SLAB_ROWS, D), jnp.float32)
    total, unused = lax.scan(add_block, start, (index_blocks, weight_blocks, grad_blocks))
    return memory_out, total.astype(jnp.bfloat16)
```

```python
import jax
import jax.numpy as jnp
import numpy as np
from jax import lax
from jax.experimental import pallas as pl
from jax.experimental.pallas import tpu as pltpu
from jax.sharding import Mesh
from jax.sharding import PartitionSpec as P


NX, NZL, NC, NY, NZH = 4, 4, 2, 4, 2
NZ = NZL * NZH
ALL = ("x", "zl", "c", "y", "zh")
FSDP = ("x", "zl", "c")
COLUMNS = 1024
VMEM_LIMIT = 20 << 20


def place(x, z, c, y):
    return (((x * NZL + z % NZL) * NC + c) * NY + y) * NZH + z // NZL


def route(dx, dz, dc):
    pairs = []
    for x in range(NX):
        for z in range(NZ):
            for c in range(NC):
                to_x, to_c = (x + dx) % NX, c ^ dc
                step = dz
                if dz == 2 and (to_x + to_c) % 2:
                    step = -2
                if dz == 3:
                    step = -1
                for y in range(NY):
                    pairs.append((place(x, z, c, y), place(to_x, (z + step) % NZ, to_c, y)))
    return pairs


def back(pairs):
    return [(b, a) for a, b in pairs]


def along_y(dy):
    return [
        (place(x, z, c, y), place(x, z, c, (y + dy) % NY))
        for x in range(NX)
        for z in range(NZ)
        for c in range(NC)
        for y in range(NY)
    ]


def other_run():
    return [
        (place(x, z, c, y), place(x, (z + NZL) % NZ, c, y))
        for x in range(NX)
        for z in range(NZ)
        for c in range(NC)
        for y in range(NY)
    ]


def in_turn(shifts):
    def load(s):
        v = np.zeros(4)
        for at, d in ((0, s[0]), (2, s[1])):
            if d == 2:
                v[at] += 1
                v[at + 1] += 1
            elif d:
                v[at if d == 1 else at + 1] += 1
        return v

    left, total, order = list(shifts), np.zeros(4), []
    while left:

        def key(s):
            t = total + load(s)
            return (t.max() - t.min(), -load(s).sum())

        best = min(left, key=key)
        left.remove(best)
        order.append(best)
        total = total + load(best)
    return order


def send(a, pairs):
    return lax.ppermute(a, ALL, pairs)


def spread(lhs, rhs, parts):
    rows = lhs.shape[0] // parts
    width = rhs[0].shape[1]

    def kernel(l_ref, *refs):
        r = jnp.concatenate([ref[...] for ref in refs[: len(rhs)]], axis=0)
        acc = jnp.dot(l_ref[...], r, preferred_element_type=jnp.float32)
        for i, out in enumerate(refs[len(rhs) :]):
            out[...] = acc[i * rows : (i + 1) * rows].astype(jnp.bfloat16)

    return pl.pallas_call(
        kernel,
        grid=(width // COLUMNS,),
        in_specs=[pl.BlockSpec(lhs.shape, lambda i: (0, 0))]
        + [pl.BlockSpec((a.shape[0], COLUMNS), lambda i: (0, i)) for a in rhs],
        out_specs=[pl.BlockSpec((rows, COLUMNS), lambda i: (0, i))] * parts,
        out_shape=[jax.ShapeDtypeStruct((rows, width), jnp.bfloat16)] * parts,
        compiler_params=pltpu.CompilerParams(vmem_limit_bytes=VMEM_LIMIT),
    )(lhs, *rhs)


def gathered(lhs, parts, stride, out_dtype):
    n, rows, width = len(parts), parts[0].shape[0], parts[0].shape[1]

    def kernel(l_ref, *refs):
        out, scratch = refs[n], refs[n + 1]
        if stride != rows:

            @pl.when(pl.program_id(0) == 0)
            def _():
                scratch[...] = jnp.zeros_like(scratch)

        for i in range(n):
            scratch[i * stride : i * stride + rows, :] = refs[i][...]
        out[...] = jnp.dot(
            l_ref[...], scratch[...], preferred_element_type=jnp.float32
        ).astype(out_dtype)

    return pl.pallas_call(
        kernel,
        grid=(width // COLUMNS,),
        in_specs=[pl.BlockSpec(lhs.shape, lambda i: (0, 0))]
        + [pl.BlockSpec((rows, COLUMNS), lambda i: (0, i))] * n,
        out_specs=pl.BlockSpec((lhs.shape[0], COLUMNS), lambda i: (0, i)),
        out_shape=jax.ShapeDtypeStruct((lhs.shape[0], width), out_dtype),
        scratch_shapes=[pltpu.VMEM((n * stride, COLUMNS), jnp.bfloat16)],
        compiler_params=pltpu.CompilerParams(vmem_limit_bytes=VMEM_LIMIT),
    )(lhs, *parts)


def body(tokens, owner, row_pick, query_weight, sub_keys, values, cotangent):
    tok_rows, width = tokens.shape
    heads = owner.shape[1]
    block_rows = values.shape[0]
    key_width = sub_keys.shape[2]
    depth = query_weight.shape[0]
    groups = NX * NZL * NC
    capacity = max(2, 3 * tok_rows * heads // (2 * groups))
    total_slots = groups * capacity
    requests = tok_rows * heads
    x, zl, c = lax.axis_index("x"), lax.axis_index("zl"), lax.axis_index("c")
    y, zh = lax.axis_index("y"), lax.axis_index("zh")
    swap = route(0, 0, 1)

    near = [send(query_weight, route(d, 0, 0)) for d in (1, 3, 2)]
    other_cotangent = send(cotangent, swap)

    own_by_head = owner.T
    way = (
        (((own_by_head >> 3) - x) & 3) * 8
        + ((((own_by_head >> 1) & 3) - zl) & 3) * 2
        + ((own_by_head & 1) ^ c)
    )
    flat_way = way.reshape(-1)
    hits = (flat_way[:, None] == jnp.arange(groups, dtype=jnp.int32)[None, :]).astype(jnp.bfloat16)
    positions = jnp.arange(requests, dtype=jnp.int32)
    lower = (positions[:, None] >= positions[None, :]).astype(jnp.bfloat16)
    counts = jnp.dot(lower, hits, preferred_element_type=jnp.float32)
    ranks = jnp.sum((counts - 1.0) * hits.astype(jnp.float32), axis=1).astype(jnp.int32)
    ranks = ranks.reshape(heads, tok_rows)
    slot = way * capacity + ranks
    crosses = (way & 1) == 1
    other_slot = send(jnp.where(crosses, slot, -1), swap)
    pair_slot = jnp.concatenate([jnp.where(crosses, -1, slot), other_slot], axis=1)
    slots = jnp.arange(total_slots, dtype=jnp.int32)
    per_token = jnp.any(slots[:, None, None] == pair_slot[None, :, :], axis=1).astype(jnp.bfloat16)

    row = jnp.zeros((NX, depth, heads * key_width), jnp.bfloat16)
    row = lax.dynamic_update_slice(row, query_weight[None], (x, 0, 0))
    for d, a in zip((1, 3, 2), near):
        row = lax.dynamic_update_slice(row, a[None], ((x - d) & 3, 0, 0))
    ways = [(dx, dz) for dx in range(NX) for dz in range(NZL)]
    chips = NX * NZL
    pieces = spread(per_token, (cotangent, other_cotangent), chips)
    turn = in_turn([w for w in ways if w != (0, 0)])
    arrived = {(0, 0): pieces[0]}

    for dx, dz in turn:
        arrived[(dx, dz)] = send(pieces[dx * NZL + dz], route(dx, dz, 0))

    half = NX // 2
    far = [
        (1, 0, send(row, route(0, 1, 0))),
        (3, 0, send(row, route(0, 3, 0))),
        (2, 0, send(row[:half], z_two(2))),
        (2, half, send(row[half:], z_two(-2))),
    ]
    own_rows = jnp.zeros((NZL, NX, depth, heads * key_width), jnp.bfloat16)
    own_rows = lax.dynamic_update_slice(own_rows, row[None], (zl, 0, 0, 0))
    for d, at, a in far:
        own_rows = lax.dynamic_update_slice(own_rows, a[None], ((zl - d) & 3, at, 0, 0))
    own_rows = own_rows.reshape(NZL * NX * depth, heads * key_width)
    other_rows = send(own_rows, swap)

    by_core = tokens.reshape(tok_rows, NX, NZL, NC, depth).transpose(3, 0, 2, 1, 4)
    by_core = by_core.reshape(NC, tok_rows, width // NC)
    query = jnp.dot(
        lax.dynamic_index_in_dim(by_core, c, keepdims=False),
        own_rows,
        preferred_element_type=jnp.float32,
    ) + jnp.dot(
        lax.dynamic_index_in_dim(by_core, 1 - c, keepdims=False),
        other_rows,
        preferred_element_type=jnp.float32,
    )
    query = query.astype(jnp.bfloat16).reshape(tok_rows, heads, key_width)
    full = jnp.einsum("thk,hrk->htr", query, sub_keys, preferred_element_type=jnp.float32)
    block = jnp.arange(block_rows, dtype=jnp.int32)
    read = jnp.any(row_pick.transpose(1, 0, 2)[:, :, :, None] == block, axis=2)
    score = full * (1.0 / key_width**0.5)
    top = jnp.max(jnp.where(read, score, -jnp.inf), axis=2, keepdims=True)
    expo = jnp.where(read, jnp.exp(jnp.where(read, score - top, 0.0)), 0.0)
    table = (expo / jnp.sum(expo, axis=2, keepdims=True)).astype(jnp.bfloat16)
    table = table.reshape(requests, block_rows)
    dispatch = (slots[:, None] == slot.reshape(1, -1)).astype(jnp.bfloat16)
    table = jnp.dot(dispatch, table, preferred_element_type=jnp.float32).astype(jnp.bfloat16)
    table = table.reshape(chips, NC, capacity, block_rows)
    table = jnp.concatenate([table[:, 0], send(table[:, 1], swap)], axis=1)
    table = table.reshape(NX, NZL, NC * capacity, block_rows)

    up = send(table[:, 1], route(0, 1, 0))
    down = send(table[:, 3], route(0, 3, 0))
    even = send(table[::2, 2], route(0, 2, 0))
    odd = send(table[1::2, 2], other_two())
    two = jnp.stack([even, odd], axis=1).reshape(table[:, 2].shape)
    table = jnp.stack([table[:, 0], up, two, down], axis=1)
    table = jnp.stack(
        [table[0]] + [send(table[dx], route(dx, 0, 0)) for dx in range(1, NX)], axis=0
    )
    table = table.reshape(total_slots, block_rows)

    sums = spread(table, (values,), groups)
    turn = in_turn(
        [(dx, dz, dc) for dx, dz in ways for dc in range(NC) if (dx, dz, dc) != (0, 0, 0)]
    )
    returned = {(0, 0, 0): sums[0]}

    for w in turn:
        dx, dz, dc = w
        returned[w] = send(sums[(dx * NZL + dz) * NC + dc], back(route(*w)))

    grad = gathered(table.T, [arrived[w] for w in ways], NC * capacity, jnp.float32)
    kept = block_rows // NY
    grad = grad.reshape(NY, kept, width)
    parts = [
        lax.dynamic_index_in_dim(grad, (y + dy) & 3, keepdims=False).astype(jnp.bfloat16)
        for dy in range(1, NY)
    ]
    total = lax.dynamic_index_in_dim(grad, y, keepdims=False)
    parts = [send(a, along_y(dy)) for dy, a in enumerate(parts, 1)]
    total = total + sum(a.astype(jnp.float32) for a in parts)
    total = total.reshape(NZH, kept // NZH, width)
    away = lax.dynamic_index_in_dim(total, 1 - zh, keepdims=False).astype(jnp.bfloat16)
    grad_values = lax.dynamic_index_in_dim(total, zh, keepdims=False)
    grad_values = grad_values + send(away, other_run()).astype(jnp.float32)

    stride = 32
    wide_slot = way * stride + ranks
    wide = jnp.arange(groups * stride, dtype=jnp.int32)
    combine = jnp.any(wide_slot.T[:, :, None] == wide[None, None, :], axis=1).astype(jnp.bfloat16)
    memory_out = gathered(
        combine,
        [returned[(dx, dz, dc)] for dx, dz in ways for dc in range(NC)],
        stride,
        jnp.bfloat16,
    )
    return memory_out, grad_values.astype(jnp.bfloat16)


def z_two(step):
    return [
        (place(x, z, c, y), place(x, (z + step) % NZ, c, y))
        for x in range(NX)
        for z in range(NZ)
        for c in range(NC)
        for y in range(NY)
    ]


def other_two():
    return back(route(0, 2, 0))


def solution(mesh):
    torus = Mesh(mesh.devices.reshape(NX, NZL, NC, NY, NZH), ALL)
    return jax.shard_map(
        body,
        mesh=torus,
        in_specs=(
            P(ALL, None),
            P(ALL, None),
            P(ALL, None, None),
            P(FSDP, None),
            P(),
            P(FSDP, None),
            P(ALL, None),
        ),
        out_specs=(P(ALL, None), P(ALL, None)),
        check_vma=False,
    )
```

```python
import jax
import jax.numpy as jnp
import numpy as np
from jax import lax
from jax.experimental import pallas as pl
from jax.experimental.pallas import tpu as pltpu
from jax.sharding import Mesh
from jax.sharding import PartitionSpec as P


NX, NZL, NC, NY, NZH = 4, 4, 2, 4, 2
NZ = NZL * NZH
ALL = ("x", "zl", "c", "y", "zh")
FSDP = ("x", "zl", "c")
COLUMNS = 1024
VMEM_LIMIT = 20 << 20


def place(x, z, c, y):
    return (((x * NZL + z % NZL) * NC + c) * NY + y) * NZH + z // NZL


def two_away(z, within):
    return (z + (2 if (z % NZL < 2) == within else -2)) % NZ


def route(dx, dz, dc):
    pairs = []
    for x in range(NX):
        for z in range(NZ):
            for c in range(NC):
                to_c = c ^ dc
                if dz == 2:
                    to_z = two_away(z, ((x + to_c) % 2 == 0) != (dx == 3))
                else:
                    to_z = (z + (-1 if dz == 3 else dz)) % NZ
                for y in range(NY):
                    pairs.append((place(x, z, c, y), place((x + dx) % NX, to_z, to_c, y)))
    return pairs


def back(pairs):
    return [(b, a) for a, b in pairs]


def along_y(dy):
    return [
        (place(x, z, c, y), place(x, z, c, (y + dy) % NY))
        for x in range(NX)
        for z in range(NZ)
        for c in range(NC)
        for y in range(NY)
    ]


def other_run():
    return [
        (place(x, z, c, y), place(x, (z + NZL) % NZ, c, y))
        for x in range(NX)
        for z in range(NZ)
        for c in range(NC)
        for y in range(NY)
    ]


def in_turn(shifts):
    def load(s):
        v = np.zeros(4)
        for at, d in ((0, s[0]), (2, s[1])):
            if d == 2:
                v[at] += 1
                v[at + 1] += 1
            elif d:
                v[at if d == 1 else at + 1] += 1
        return v

    left, total, order = list(shifts), np.zeros(4), []
    while left:

        def key(s):
            t = total + load(s)
            return (t.max() - t.min(), -load(s).sum())

        best = min(left, key=key)
        left.remove(best)
        order.append(best)
        total = total + load(best)
    return order


def send(a, pairs):
    return lax.ppermute(a, ALL, pairs)


def spread(lhs, rhs, parts):
    rows = lhs.shape[0] // parts
    width = rhs[0].shape[1]

    def kernel(l_ref, *refs):
        r = jnp.concatenate([ref[...] for ref in refs[: len(rhs)]], axis=0)
        acc = jnp.dot(l_ref[...], r, preferred_element_type=jnp.float32)
        for i, out in enumerate(refs[len(rhs) :]):
            out[...] = acc[i * rows : (i + 1) * rows].astype(jnp.bfloat16)

    return pl.pallas_call(
        kernel,
        grid=(width // COLUMNS,),
        in_specs=[pl.BlockSpec(lhs.shape, lambda i: (0, 0))]
        + [pl.BlockSpec((a.shape[0], COLUMNS), lambda i: (0, i)) for a in rhs],
        out_specs=[pl.BlockSpec((rows, COLUMNS), lambda i: (0, i))] * parts,
        out_shape=[jax.ShapeDtypeStruct((rows, width), jnp.bfloat16)] * parts,
        compiler_params=pltpu.CompilerParams(vmem_limit_bytes=VMEM_LIMIT),
    )(lhs, *rhs)


def gathered(lhs, parts, stride, out_dtype):
    n, rows, width = len(parts), parts[0].shape[0], parts[0].shape[1]

    def kernel(l_ref, *refs):
        out, scratch = refs[n], refs[n + 1]
        if stride != rows:

            @pl.when(pl.program_id(0) == 0)
            def _():
                scratch[...] = jnp.zeros_like(scratch)

        for i in range(n):
            scratch[i * stride : i * stride + rows, :] = refs[i][...]
        out[...] = jnp.dot(
            l_ref[...], scratch[...], preferred_element_type=jnp.float32
        ).astype(out_dtype)

    return pl.pallas_call(
        kernel,
        grid=(width // COLUMNS,),
        in_specs=[pl.BlockSpec(lhs.shape, lambda i: (0, 0))]
        + [pl.BlockSpec((rows, COLUMNS), lambda i: (0, i))] * n,
        out_specs=pl.BlockSpec((lhs.shape[0], COLUMNS), lambda i: (0, i)),
        out_shape=jax.ShapeDtypeStruct((lhs.shape[0], width), out_dtype),
        scratch_shapes=[pltpu.VMEM((n * stride, COLUMNS), jnp.bfloat16)],
        compiler_params=pltpu.CompilerParams(vmem_limit_bytes=VMEM_LIMIT),
    )(lhs, *parts)


def body(tokens, owner, row_pick, query_weight, sub_keys, values, cotangent):
    tok_rows, width = tokens.shape
    heads = owner.shape[1]
    block_rows = values.shape[0]
    key_width = sub_keys.shape[2]
    depth = query_weight.shape[0]
    groups = NX * NZL * NC
    capacity = max(2, 3 * tok_rows * heads // (2 * groups))
    total_slots = groups * capacity
    requests = tok_rows * heads
    x, zl, c = lax.axis_index("x"), lax.axis_index("zl"), lax.axis_index("c")
    y, zh = lax.axis_index("y"), lax.axis_index("zh")
    swap = route(0, 0, 1)

    near = [send(query_weight, route(d, 0, 0)) for d in (1, 3, 2)]
    other_cotangent = send(cotangent, swap)

    own_by_head = owner.T
    way = (
        (((own_by_head >> 3) - x) & 3) * 8
        + ((((own_by_head >> 1) & 3) - zl) & 3) * 2
        + ((own_by_head & 1) ^ c)
    )
    flat_way = way.reshape(-1)
    hits = (flat_way[:, None] == jnp.arange(groups, dtype=jnp.int32)[None, :]).astype(jnp.bfloat16)
    positions = jnp.arange(requests, dtype=jnp.int32)
    lower = (positions[:, None] >= positions[None, :]).astype(jnp.bfloat16)
    counts = jnp.dot(lower, hits, preferred_element_type=jnp.float32)
    ranks = jnp.sum((counts - 1.0) * hits.astype(jnp.float32), axis=1).astype(jnp.int32)
    ranks = ranks.reshape(heads, tok_rows)
    slot = way * capacity + ranks
    crosses = (way & 1) == 1
    other_slot = send(jnp.where(crosses, slot, -1), swap)
    pair_slot = jnp.concatenate([jnp.where(crosses, -1, slot), other_slot], axis=1)
    slots = jnp.arange(total_slots, dtype=jnp.int32)
    per_token = jnp.any(slots[:, None, None] == pair_slot[None, :, :], axis=1).astype(jnp.bfloat16)

    row = jnp.zeros((NX, depth, heads * key_width), jnp.bfloat16)
    row = lax.dynamic_update_slice(row, query_weight[None], (x, 0, 0))
    for d, a in zip((1, 3, 2), near):
        row = lax.dynamic_update_slice(row, a[None], ((x - d) & 3, 0, 0))
    ways = [(dx, dz) for dx in range(NX) for dz in range(NZL)]
    chips = NX * NZL
    pieces = spread(per_token, (cotangent, other_cotangent), chips)
    turn = in_turn([w for w in ways if w != (0, 0)])
    arrived = {(0, 0): pieces[0]}

    for dx, dz in turn:
        arrived[(dx, dz)] = send(pieces[dx * NZL + dz], route(dx, dz, 0))

    far = [(dz, send(row, route(0, dz, 0))) for dz in (1, 3, 2)]
    own_rows = jnp.zeros((NZL, NX, depth, heads * key_width), jnp.bfloat16)
    own_rows = lax.dynamic_update_slice(own_rows, row[None], (zl, 0, 0, 0))
    for d, a in far:
        own_rows = lax.dynamic_update_slice(own_rows, a[None], ((zl - d) & 3, 0, 0, 0))
    own_rows = own_rows.reshape(NZL * NX * depth, heads * key_width)
    other_rows = send(own_rows, swap)

    by_core = tokens.reshape(tok_rows, NX, NZL, NC, depth).transpose(3, 0, 2, 1, 4)
    by_core = by_core.reshape(NC, tok_rows, width // NC)
    query = jnp.dot(
        lax.dynamic_index_in_dim(by_core, c, keepdims=False),
        own_rows,
        preferred_element_type=jnp.float32,
    ) + jnp.dot(
        lax.dynamic_index_in_dim(by_core, 1 - c, keepdims=False),
        other_rows,
        preferred_element_type=jnp.float32,
    )
    query = query.astype(jnp.bfloat16).reshape(tok_rows, heads, key_width)
    full = jnp.einsum("thk,hrk->htr", query, sub_keys, preferred_element_type=jnp.float32)
    block = jnp.arange(block_rows, dtype=jnp.int32)
    read = jnp.any(row_pick.transpose(1, 0, 2)[:, :, :, None] == block, axis=2)
    score = full * (1.0 / key_width**0.5)
    top = jnp.max(jnp.where(read, score, -jnp.inf), axis=2, keepdims=True)
    expo = jnp.where(read, jnp.exp(jnp.where(read, score - top, 0.0)), 0.0)
    table = (expo / jnp.sum(expo, axis=2, keepdims=True)).astype(jnp.bfloat16)
    table = table.reshape(requests, block_rows)
    dispatch = (slots[:, None] == slot.reshape(1, -1)).astype(jnp.bfloat16)
    table = jnp.dot(dispatch, table, preferred_element_type=jnp.float32).astype(jnp.bfloat16)
    table = table.reshape(chips, NC, capacity, block_rows)
    table = jnp.concatenate([table[:, 0], send(table[:, 1], swap)], axis=1)
    table = table.reshape(NX, NZL, NC * capacity, block_rows)

    two = send(table[:3, 2], route(0, 2, 0))
    up = send(table[:, 1], route(0, 1, 0))
    down = send(table[:, 3], route(0, 3, 0))
    alone = send(table[3, 2], route(3, 2, 0))
    three = jnp.stack([table[:, 0], up, down], axis=1)
    near_x = [
        jnp.concatenate([three[dx], two[dx][None]], axis=0) if dx < 3 else three[dx]
        for dx in range(NX)
    ]
    near_x = [near_x[0]] + [send(near_x[dx], route(dx, 0, 0)) for dx in range(1, NX)]
    near_x[3] = jnp.concatenate([near_x[3], alone[None]], axis=0)
    table = jnp.stack(near_x, axis=0)
    zs = (0, 1, 3, 2)
    ways = [(dx, dz) for dx in range(NX) for dz in zs]
    table = table.reshape(total_slots, block_rows)

    sums = spread(table, (values,), groups)
    turn = in_turn(
        [(dx, dz, dc) for dx, dz in ways for dc in range(NC) if (dx, dz, dc) != (0, 0, 0)]
    )
    returned = {(0, 0, 0): sums[0]}

    for w in turn:
        dx, dz, dc = w
        returned[w] = send(sums[(dx * NZL + zs.index(dz)) * NC + dc], back(route(*w)))

    grad = gathered(table.T, [arrived[w] for w in ways], NC * capacity, jnp.float32)
    kept = block_rows // NY
    grad = grad.reshape(NY, kept, width)
    parts = [
        lax.dynamic_index_in_dim(grad, (y + dy) & 3, keepdims=False).astype(jnp.bfloat16)
        for dy in range(1, NY)
    ]
    total = lax.dynamic_index_in_dim(grad, y, keepdims=False)
    parts = [send(a, along_y(dy)) for dy, a in enumerate(parts, 1)]
    total = total + sum(a.astype(jnp.float32) for a in parts)
    total = total.reshape(NZH, kept // NZH, width)
    away = lax.dynamic_index_in_dim(total, 1 - zh, keepdims=False).astype(jnp.bfloat16)
    grad_values = lax.dynamic_index_in_dim(total, zh, keepdims=False)
    grad_values = grad_values + send(away, other_run()).astype(jnp.float32)

    stride = 32
    wide_slot = way * stride + ranks
    wide = jnp.arange(groups * stride, dtype=jnp.int32)
    combine = jnp.any(wide_slot.T[:, :, None] == wide[None, None, :], axis=1).astype(jnp.bfloat16)
    memory_out = gathered(
        combine,
        [returned[(dx, dz, dc)] for dx in range(NX) for dz in range(NZL) for dc in range(NC)],
        stride,
        jnp.bfloat16,
    )
    return memory_out, grad_values.astype(jnp.bfloat16)


def solution(mesh):
    torus = Mesh(mesh.devices.reshape(NX, NZL, NC, NY, NZH), ALL)
    return jax.shard_map(
        body,
        mesh=torus,
        in_specs=(
            P(ALL, None),
            P(ALL, None),
            P(ALL, None, None),
            P(FSDP, None),
            P(),
            P(FSDP, None),
            P(ALL, None),
        ),
        out_specs=(P(ALL, None), P(ALL, None)),
        check_vma=False,
    )
```

```python
import jax
import jax.numpy as jnp
import numpy as np
from jax import lax
from jax.experimental import pallas as pl
from jax.experimental.pallas import tpu as pltpu
from jax.sharding import Mesh
from jax.sharding import PartitionSpec as P


NX, NZL, NC, NY, NZH = 4, 4, 2, 4, 2
NZ = NZL * NZH
ALL = ("x", "zl", "c", "y", "zh")
FSDP = ("x", "zl", "c")
COLUMNS = 1024
VMEM_LIMIT = 12 << 20


def place(x, z, c, y):
    return (((x * NZL + z % NZL) * NC + c) * NY + y) * NZH + z // NZL


def two_away(z, within):
    return (z + (2 if (z % NZL < 2) == within else -2)) % NZ


def route(dx, dz, dc):
    pairs = []
    for x in range(NX):
        for z in range(NZ):
            for c in range(NC):
                to_c = c ^ dc
                if dz == 2:
                    to_z = two_away(z, ((x + to_c) % 2 == 0) != (dx == 3))
                else:
                    to_z = (z + (-1 if dz == 3 else dz)) % NZ
                for y in range(NY):
                    pairs.append((place(x, z, c, y), place((x + dx) % NX, to_z, to_c, y)))
    return pairs


def back(pairs):
    return [(b, a) for a, b in pairs]


def along_y(dy):
    return [
        (place(x, z, c, y), place(x, z, c, (y + dy) % NY))
        for x in range(NX)
        for z in range(NZ)
        for c in range(NC)
        for y in range(NY)
    ]


def other_run():
    return [
        (place(x, z, c, y), place(x, (z + NZL) % NZ, c, y))
        for x in range(NX)
        for z in range(NZ)
        for c in range(NC)
        for y in range(NY)
    ]


def in_turn(shifts):
    def load(s):
        v = np.zeros(4)
        for at, d in ((0, s[0]), (2, s[1])):
            if d == 2:
                v[at] += 1
                v[at + 1] += 1
            elif d:
                v[at if d == 1 else at + 1] += 1
        return v

    left, total, order = list(shifts), np.zeros(4), []
    while left:

        def key(s):
            t = total + load(s)
            return (t.max() - t.min(), -load(s).sum())

        best = min(left, key=key)
        left.remove(best)
        order.append(best)
        total = total + load(best)
    return order


def send(a, pairs):
    return lax.ppermute(a, ALL, pairs)


def spread(lhs, rhs, parts):
    rows = lhs.shape[0] // parts
    width = rhs[0].shape[1]

    def kernel(l_ref, *refs):
        r = jnp.concatenate([ref[...] for ref in refs[: len(rhs)]], axis=0)
        acc = jnp.dot(l_ref[...], r, preferred_element_type=jnp.float32)
        for i, out in enumerate(refs[len(rhs) :]):
            out[...] = acc[i * rows : (i + 1) * rows].astype(jnp.bfloat16)

    return pl.pallas_call(
        kernel,
        grid=(width // COLUMNS,),
        in_specs=[pl.BlockSpec(lhs.shape, lambda i: (0, 0))]
        + [pl.BlockSpec((a.shape[0], COLUMNS), lambda i: (0, i)) for a in rhs],
        out_specs=[pl.BlockSpec((rows, COLUMNS), lambda i: (0, i))] * parts,
        out_shape=[pltpu.HBM((rows, width), jnp.bfloat16)] * parts,
        compiler_params=pltpu.CompilerParams(vmem_limit_bytes=VMEM_LIMIT),
    )(lhs, *rhs)


def gathered(lhs, parts, out_dtypes, first=0, blocks=None):
    n, rows, width = len(parts), parts[0].shape[0], parts[0].shape[1]
    blocks = blocks or width // COLUMNS
    share = lhs.shape[0] // len(out_dtypes)

    def kernel(l_ref, *refs):
        outs, scratch = refs[n:-1], refs[-1]
        for i in range(n):
            scratch[i * rows : (i + 1) * rows, :] = refs[i][...]
        acc = jnp.dot(l_ref[...], scratch[...], preferred_element_type=jnp.float32)
        for i, out in enumerate(outs):
            out[...] = acc[i * share : (i + 1) * share].astype(out.dtype)

    return pl.pallas_call(
        kernel,
        grid=(blocks,),
        in_specs=[pl.BlockSpec(lhs.shape, lambda i: (0, 0))]
        + [pl.BlockSpec((rows, COLUMNS), lambda i: (0, first + i))] * n,
        out_specs=[pl.BlockSpec((share, COLUMNS), lambda i: (0, i))] * len(out_dtypes),
        out_shape=[jax.ShapeDtypeStruct((share, blocks * COLUMNS), d) for d in out_dtypes],
        scratch_shapes=[pltpu.VMEM((n * rows, COLUMNS), jnp.bfloat16)],
        compiler_params=pltpu.CompilerParams(vmem_limit_bytes=VMEM_LIMIT),
    )(lhs, *parts)


def both_halves(arrays):
    rows, half = arrays[0].shape

    def kernel(left, left_other, right, right_other, out):
        out[:, :half] = (left[...] + left_other[...].astype(jnp.float32)).astype(out.dtype)
        out[:, half:] = (right[...] + right_other[...].astype(jnp.float32)).astype(out.dtype)

    return pl.pallas_call(
        kernel,
        name="halves",
        out_shape=jax.ShapeDtypeStruct((rows, 2 * half), jnp.bfloat16),
        compiler_params=pltpu.CompilerParams(vmem_limit_bytes=VMEM_LIMIT),
    )(*arrays)


def body(tokens, owner, row_pick, query_weight, sub_keys, values, cotangent):
    tok_rows, width = tokens.shape
    heads = owner.shape[1]
    block_rows = values.shape[0]
    key_width = sub_keys.shape[2]
    depth = query_weight.shape[0]
    groups = NX * NZL * NC
    capacity = max(2, 3 * tok_rows * heads // (2 * groups))
    total_slots = groups * capacity
    requests = tok_rows * heads
    x, zl, c = lax.axis_index("x"), lax.axis_index("zl"), lax.axis_index("c")
    y, zh = lax.axis_index("y"), lax.axis_index("zh")
    swap = route(0, 0, 1)

    near = [send(query_weight, route(d, 0, 0)) for d in (1, 3, 2)]
    other_cotangent = send(cotangent, swap)

    own_by_head = owner.T
    way = (
        (((own_by_head >> 3) - x) & 3) * 8
        + ((((own_by_head >> 1) & 3) - zl) & 3) * 2
        + ((own_by_head & 1) ^ c)
    )
    flat_way = way.reshape(-1)
    hits = (flat_way[:, None] == jnp.arange(groups, dtype=jnp.int32)[None, :]).astype(jnp.bfloat16)
    positions = jnp.arange(requests, dtype=jnp.int32)
    lower = (positions[:, None] >= positions[None, :]).astype(jnp.bfloat16)
    counts = jnp.dot(lower, hits, preferred_element_type=jnp.float32)
    ranks = jnp.sum((counts - 1.0) * hits.astype(jnp.float32), axis=1).astype(jnp.int32)
    ranks = ranks.reshape(heads, tok_rows)
    slot = way * capacity + ranks
    crosses = (way & 1) == 1
    other_slot = send(jnp.where(crosses, slot, -1), swap)
    pair_slot = jnp.concatenate([jnp.where(crosses, -1, slot), other_slot], axis=1)
    slots = jnp.arange(total_slots, dtype=jnp.int32)
    per_token = jnp.any(slots[:, None, None] == pair_slot[None, :, :], axis=1).astype(jnp.bfloat16)

    row = jnp.zeros((NX, depth, heads * key_width), jnp.bfloat16)
    row = lax.dynamic_update_slice(row, query_weight[None], (x, 0, 0))
    for d, a in zip((1, 3, 2), near):
        row = lax.dynamic_update_slice(row, a[None], ((x - d) & 3, 0, 0))
    ways = [(dx, dz) for dx in range(NX) for dz in range(NZL)]
    chips = NX * NZL
    pieces = spread(per_token, (cotangent, other_cotangent), chips)
    turn = in_turn([w for w in ways if w != (0, 0)])
    arrived = {(0, 0): pieces[0]}

    for dx, dz in turn:
        arrived[(dx, dz)] = send(pieces[dx * NZL + dz], route(dx, dz, 0))

    quarter = lax.dynamic_index_in_dim(row, y, keepdims=False)
    far = [send(quarter, route(0, dz, 0)) for dz in (1, 3, 2)]
    three = jnp.stack(far, axis=0)
    across = [three] + [send(three, along_y(dy)) for dy in (1, 3, 2)]
    own_rows = jnp.zeros((NZL, NX, depth, heads * key_width), jnp.bfloat16)
    own_rows = lax.dynamic_update_slice(own_rows, row[None], (zl, 0, 0, 0))
    for dy, group in zip((0, 1, 3, 2), across):
        for i, dz in enumerate((1, 3, 2)):
            own_rows = lax.dynamic_update_slice(
                own_rows, group[i][None, None], ((zl - dz) & 3, (y - dy) & 3, 0, 0)
            )
    own_rows = own_rows.reshape(NZL * NX * depth, heads * key_width)
    other_rows = send(own_rows, swap)

    by_core = tokens.reshape(tok_rows, NX, NZL, NC, depth).transpose(3, 0, 2, 1, 4)
    by_core = by_core.reshape(NC, tok_rows, width // NC)
    query = jnp.dot(
        lax.dynamic_index_in_dim(by_core, c, keepdims=False),
        own_rows,
        preferred_element_type=jnp.float32,
    ) + jnp.dot(
        lax.dynamic_index_in_dim(by_core, 1 - c, keepdims=False),
        other_rows,
        preferred_element_type=jnp.float32,
    )
    query = query.astype(jnp.bfloat16).reshape(tok_rows, heads, key_width)
    full = jnp.einsum("thk,hrk->htr", query, sub_keys, preferred_element_type=jnp.float32)
    block = jnp.arange(block_rows, dtype=jnp.int32)
    read = jnp.any(row_pick.transpose(1, 0, 2)[:, :, :, None] == block, axis=2)
    score = full * (1.0 / key_width**0.5)
    top = jnp.max(jnp.where(read, score, -jnp.inf), axis=2, keepdims=True)
    expo = jnp.where(read, jnp.exp(jnp.where(read, score - top, 0.0)), 0.0)
    table = (expo / jnp.sum(expo, axis=2, keepdims=True)).astype(jnp.bfloat16)
    table = table.reshape(requests, block_rows)
    dispatch = (slots[:, None] == slot.reshape(1, -1)).astype(jnp.bfloat16)
    table = jnp.dot(dispatch, table, preferred_element_type=jnp.float32).astype(jnp.bfloat16)
    table = table.reshape(chips, NC, capacity, block_rows)
    table = jnp.concatenate([table[:, 0], send(table[:, 1], swap)], axis=1)
    table = table.reshape(NX, NZL, NC * capacity, block_rows)

    two = send(table[:3, 2], route(0, 2, 0))
    up = send(table[:, 1], route(0, 1, 0))
    down = send(table[:, 3], route(0, 3, 0))
    alone = send(table[3, 2], route(3, 2, 0))
    three = jnp.stack([table[:, 0], up, down], axis=1)
    near_x = [
        jnp.concatenate([three[dx], two[dx][None]], axis=0) if dx < 3 else three[dx]
        for dx in range(NX)
    ]
    near_x = [near_x[0]] + [send(near_x[dx], route(dx, 0, 0)) for dx in range(1, NX)]
    near_x[3] = jnp.concatenate([near_x[3], alone[None]], axis=0)
    table = jnp.stack(near_x, axis=0)
    zs = (0, 1, 3, 2)
    ways = [(dx, dz) for dx in range(NX) for dz in zs]
    table = table.reshape(total_slots, block_rows)

    sums = spread(table, (values,), chips)
    returned = {(0, 0): sums[0]}
    for dx, dz in turn:
        sent = sums[dx * NZL + zs.index(dz)]
        returned[(dx, dz)] = send(sent, back(route(dx, dz, 0)))

    (grad,) = gathered(table.T, [arrived[w] for w in ways], (jnp.float32,))
    kept = block_rows // NY
    grad = grad.reshape(NY, kept, width)
    parts = [
        lax.dynamic_index_in_dim(grad, (y + dy) & 3, keepdims=False).astype(jnp.bfloat16)
        for dy in range(1, NY)
    ]
    total = lax.dynamic_index_in_dim(grad, y, keepdims=False)
    parts = [send(a, along_y(dy)) for dy, a in enumerate(parts, 1)]
    total = total + sum(a.astype(jnp.float32) for a in parts)
    total = total.reshape(NZH, kept // NZH, width)
    away = lax.dynamic_index_in_dim(total, 1 - zh, keepdims=False).astype(jnp.bfloat16)
    grad_values = lax.dynamic_index_in_dim(total, zh, keepdims=False)
    grad_values = grad_values + send(away, other_run()).astype(jnp.float32)

    combine = jnp.any(pair_slot.T[:, :, None] == slots[None, None, :], axis=1)
    combine = combine.astype(jnp.bfloat16)
    came = [returned[(dx, dz)] for dx in range(NX) for dz in range(NZL)]
    memory_out = []
    blocks = width // COLUMNS
    for i in range(2):
        own, other = gathered(
            combine, came, (jnp.float32, jnp.bfloat16), i * (blocks // 2), blocks // 2
        )
        memory_out += [own, send(other, swap)]
    return both_halves(memory_out), grad_values.astype(jnp.bfloat16)


def solution(mesh):
    torus = Mesh(mesh.devices.reshape(NX, NZL, NC, NY, NZH), ALL)
    return jax.shard_map(
        body,
        mesh=torus,
        in_specs=(
            P(ALL, None),
            P(ALL, None),
            P(ALL, None, None),
            P(FSDP, None),
            P(),
            P(FSDP, None),
            P(ALL, None),
        ),
        out_specs=(P(ALL, None), P(ALL, None)),
        check_vma=False,
    )
```
